32 devices in a mesh: gx: 4 (over x, core), gy: 8 (over z, y).
Axes of the slice: x: 2, y: 2, z: 4, core: 2. Of those that a mesh axis runs over, the one named last changes fastest.
Arguments:
- sources: float32 [8, 4, 256, 1024], P('gy', 'gx'), may hold values from -6 to 6
- coeff_in: bfloat16 [8, 4, 256, 256], P('gy', 'gx'), may hold values from -0.375 to 0.375
- transfer: bfloat16 [8, 8, 4, 256, 512], P(None, 'gy', 'gx'), may hold values from -0.25 to 0.25
- coeff_out: bfloat16 [8, 4, 256, 256], P('gy', 'gx'), may hold values from -0.375 to 0.375
Outputs:
- targets: float32 [8, 4, 256, 1024], P('gy', 'gx')
The draws below stay inside these ranges and needn't reach their ends.
All inputs are finite; a program needn't handle non-finite values.
Results may differ from the reference program's by a relative error of at most 0.015.
Values may be sent and summed in bfloat16 or wider, within the bound.
A program may use at most 64 MiB of HBM per device.

```python
import jax
import jax.numpy as jnp
from jax import lax

RANK = 256
LEAF = 256
COLS = 1024
LEVELS = 8
N_GX = 4
N_GY = 8


def level_of(key, shape, pieces, smallest, top_value):
    def one(dim, shards_of):
        heights = jax.random.uniform(jax.random.fold_in(jax.random.fold_in(key, 6), dim), (shards_of,), jnp.float32, smallest / len(pieces), top_value / len(pieces))
        return jnp.repeat(jnp.exp(heights), shape[dim] // shards_of).reshape((-1,) + (1,) * (len(shape) - dim - 1))

    factor_of = one(*pieces[0])
    for cut in pieces[1:]:
        factor_of = factor_of * one(*cut)
    return factor_of


def noise(stream_key, dims, width, most, pieces=(), held_as=jnp.bfloat16):
    loudness = level_of(stream_key, dims, pieces, -0.22, 0.18) if pieces else 1.0
    entries = jax.random.normal(stream_key, dims, jnp.float32) * width * loudness
    return jnp.minimum(jnp.maximum(entries, -most), most).astype(held_as)


def setup_inputs(seed: int = 0) -> dict:
    key_list = jax.random.split(jax.random.key(seed), 5)
    sources = noise(key_list[0], (N_GY, N_GX, LEAF, COLS), 1.0, 6.0, ((0, 8), (1, 4)), jnp.float32)
    coeff_in = noise(key_list[1], (N_GY, N_GX, RANK, LEAF), LEAF ** -0.5, 0.375, ((0, 8), (1, 4)))
    transfer = noise(key_list[2], (LEVELS, N_GY, N_GX, RANK, 2 * RANK), (2 * RANK) ** -0.5, 0.25, ((1, 8), (2, 4)))
    coeff_out = noise(key_list[3], (N_GY, N_GX, LEAF, RANK), RANK ** -0.5, 0.375, ((0, 8), (1, 4)))
    return {"sources": sources, "coeff_in": coeff_in, "transfer": transfer, "coeff_out": coeff_out}


def apply_level(state, weights, level_bit):
    total = state.shape[0]
    block = 1 << level_bit
    groups = total // (2 * block)
    rank_rows = state.shape[1]
    cols_count = state.shape[2]
    shaped = state.reshape(groups, 2, block, rank_rows, cols_count)
    paired = jnp.concatenate([shaped[:, 0], shaped[:, 1]], axis=-2)
    paired = paired.reshape(groups * block, 2 * rank_rows, cols_count)
    wshape = weights.reshape(groups, 2, block, rank_rows, 2 * rank_rows)
    wshape = jnp.transpose(wshape, (0, 2, 1, 3, 4)).reshape(groups * block, 2 * rank_rows, 2 * rank_rows)

    def one_pair(items):
        return jnp.dot(items[0], items[1], preferred_element_type=jnp.float32).astype(jnp.bfloat16)

    result = lax.map(one_pair, (wshape, paired))
    result = result.reshape(groups, block, 2, rank_rows, cols_count)
    result = jnp.transpose(result, (0, 2, 1, 3, 4))
    return result.reshape(total, rank_rows, cols_count)


def reference(sources, coeff_in, transfer, coeff_out):
    total = N_GX * N_GY
    nbits = total.bit_length() - 1
    leaf_rows = sources.shape[2]
    cols_count = sources.shape[3]
    rank_rows = coeff_in.shape[2]
    source_flat = sources.reshape(total, leaf_rows, cols_count).astype(jnp.bfloat16)
    inward = coeff_in.reshape(total, rank_rows, leaf_rows)

    def compress(items):
        return jnp.dot(items[0], items[1], preferred_element_type=jnp.float32).astype(jnp.bfloat16)

    state = lax.map(compress, (inward, source_flat))
    for level in range(LEVELS):
        level_bit = nbits - 1 - (level % nbits)
        weights = transfer[level].reshape(total, rank_rows, 2 * rank_rows)
        state = apply_level(state, weights, level_bit)
    outward = coeff_out.reshape(total, leaf_rows, rank_rows)

    def expand(items):
        return jnp.dot(items[0], items[1], preferred_element_type=jnp.float32)

    result = lax.map(expand, (outward, state))
    return result.reshape(N_GY, N_GX, leaf_rows, cols_count)
```

```python
import functools

import jax
import jax.numpy as jnp
from jax import lax
from jax.experimental import pallas as pl
from jax.experimental.pallas import tpu as pltpu
from jax.sharding import PartitionSpec as P

MESH = pl.DeviceIdType.MESH
WIDTH = 128
LAGS = (0, 2.1, 3.9, 5.3, 6.7, 7.4, 9.5, 11.3, 12.7)


def kernel(
    low_bits,
    nbits,
    sources,
    coeff_in,
    transfer,
    targets,
    src,
    inward,
    weights,
    pairs,
    load_sem,
    src_sem,
    out_sem,
    send_sem,
    recv_sem,
):
    levels = transfer.shape[0]
    rank = coeff_in.shape[0]
    chunks = sources.shape[1] // WIDTH
    axes = {"gx": lax.axis_index("gx"), "gy": lax.axis_index("gy")}

    def place(level):
        bit = nbits - 1 - level % nbits
        axis, mask = ("gx", 2**bit) if bit < low_bits else ("gy", 2 ** (bit - low_bits))
        index = axes[axis]
        side = index // mask % 2
        return side, {axis: index + mask * (1 - 2 * side)}

    places = [place(level) for level in range(levels)]

    def load_source(k):
        cols = pl.ds(k * WIDTH, WIDTH)
        return pltpu.make_async_copy(sources.at[:, cols], src.at[k], src_sem.at[k])

    def load_weights(level):
        return pltpu.make_async_copy(transfer.at[level], weights.at[level], load_sem.at[level])

    load_inward = pltpu.make_async_copy(coeff_in, inward, load_sem.at[levels])

    def exchange(level, k):
        side, partner = places[level]
        half = pairs.at[level, k, pl.ds(pl.multiple_of(side * rank, rank), rank), :]
        return pltpu.make_async_remote_copy(
            src_ref=half,
            dst_ref=half,
            send_sem=send_sem.at[level, k],
            recv_sem=recv_sem.at[level, k],
            device_id=partner,
            device_id_type=MESH,
        )

    barrier = pltpu.get_barrier_semaphore()
    distinct = range(min(levels, nbits))
    for level in distinct:
        pl.semaphore_signal(barrier, inc=1, device_id=places[level][1], device_id_type=MESH)

    load_inward.start()
    for k in range(chunks):
        load_source(k).start()
    for level in range(levels):
        load_weights(level).start()

    def emit(level, k, total):
        side = places[level][0]
        pairs[level, k, pl.ds(pl.multiple_of(side * rank, rank), rank), :] = total.astype(jnp.bfloat16)
        if (level, k) == (0, 0):
            pl.semaphore_wait(barrier, len(distinct))
        exchange(level, k).start()

    def stage(s, k):
        if s == 0:
            load_source(k).wait()
            total = jnp.dot(
                inward[...], src[k].astype(jnp.bfloat16), preferred_element_type=jnp.float32
            )
            emit(0, k, total)
            return
        level = s - 1
        exchange(level, k).wait_recv()
        total = jnp.dot(weights[level], pairs[level, k], preferred_element_type=jnp.float32)
        if s < levels:
            emit(s, k, total)
            return
        targets[:, k * WIDTH : (k + 1) * WIDTH] = total.astype(jnp.bfloat16)

    turns = sorted((k + LAGS[s], -s, k) for s in range(levels + 1) for k in range(chunks))
    for _, minus, k in turns:
        s = -minus
        if k == 0:
            if s == 0:
                load_inward.wait()
            else:
                load_weights(s - 1).wait()
        stage(s, k)

    for k in range(chunks):
        for level in range(levels):
            exchange(level, k).wait_send()


def expand(state, outward, targets, held, out_sem):
    width = 256
    stores = []
    for k in range(state.shape[1] // width):
        cols = pl.ds(k * width, width)
        held[:, cols] = jnp.dot(outward[...], state[:, cols], preferred_element_type=jnp.float32)
        store = pltpu.make_async_copy(held.at[:, cols], targets.at[:, cols], out_sem.at[k])
        store.start()
        stores.append(store)
    for store in stores:
        store.wait()


def body(sources, coeff_in, transfer, coeff_out):
    low_bits = lax.axis_size("gx").bit_length() - 1
    nbits = low_bits + lax.axis_size("gy").bit_length() - 1
    levels, rank = transfer.shape[0], coeff_in.shape[2]
    leaf, cols = sources.shape[2:]
    chunks = cols // WIDTH
    result = pl.pallas_call(
        functools.partial(kernel, low_bits, nbits),
        out_shape=pltpu.VMEM((rank, cols), jnp.bfloat16),
        in_specs=[pl.BlockSpec(memory_space=pl.ANY)] * 3,
        out_specs=pl.BlockSpec(memory_space=pltpu.VMEM),
        scratch_shapes=[
            pltpu.VMEM((chunks, leaf, WIDTH), jnp.float32),
            pltpu.VMEM((rank, leaf), jnp.bfloat16),
            pltpu.VMEM((levels, rank, 2 * rank), jnp.bfloat16),
            pltpu.VMEM((levels, chunks, 2 * rank, WIDTH), jnp.bfloat16),
            pltpu.SemaphoreType.DMA((levels + 2,)),
            pltpu.SemaphoreType.DMA((chunks,)),
            pltpu.SemaphoreType.DMA((chunks,)),
            pltpu.SemaphoreType.DMA((levels, chunks)),
            pltpu.SemaphoreType.DMA((levels, chunks)),
        ],
        compiler_params=pltpu.CompilerParams(collective_id=0, has_side_effects=True),
        name="butterfly",
    )(sources[0, 0], coeff_in[0, 0], transfer[:, 0, 0])
    result = pl.pallas_call(
        expand,
        out_shape=jax.ShapeDtypeStruct((leaf, cols), jnp.float32),
        in_specs=[pl.BlockSpec(memory_space=pltpu.VMEM)] * 2,
        out_specs=pl.BlockSpec(memory_space=pl.ANY),
        scratch_shapes=[
            pltpu.VMEM((leaf, cols), jnp.float32),
            pltpu.SemaphoreType.DMA((cols // 256,)),
        ],
        name="expand",
    )(pltpu.with_memory_space_constraint(result, pltpu.VMEM), pltpu.with_memory_space_constraint(coeff_out[0, 0], pltpu.VMEM))
    return result[None, None]


def solution(mesh):
    placed = (
        P("gy", "gx", None, None),
        P("gy", "gx", None, None),
        P(None, "gy", "gx", None, None),
        P("gy", "gx", None, None),
    )
    return jax.shard_map(
        body, mesh=mesh, in_specs=placed, out_specs=P("gy", "gx", None, None), check_vma=False
    )
```

```python
import functools

import jax
import jax.numpy as jnp
from jax import lax
from jax.experimental import pallas as pl
from jax.experimental.pallas import tpu as pltpu
from jax.sharding import PartitionSpec as P

MESH = pl.DeviceIdType.MESH
WIDTH = 128
LAGS = (0, 2.1, 3.9, 5.3, 6.7, 7.4, 9.5, 11.3, 12.7)


def timetable(blocks):
    return [((k, None), float(k)) for k in range(blocks)]


def kernel(
    low_bits,
    nbits,
    sources,
    coeff_in,
    transfer,
    state,
    src,
    inward,
    weights,
    pairs,
    load_sem,
    src_sem,
    send_sem,
    recv_sem,
):
    levels = transfer.shape[0]
    rank = coeff_in.shape[0]
    blocks = sources.shape[1] // WIDTH
    axes = {"gx": lax.axis_index("gx"), "gy": lax.axis_index("gy")}

    def place(level):
        bit = nbits - 1 - level % nbits
        axis, mask = ("gx", 2**bit) if bit < low_bits else ("gy", 2 ** (bit - low_bits))
        index = axes[axis]
        side = index // mask % 2
        return side, {axis: index + mask * (1 - 2 * side)}

    pieces = timetable(blocks)
    slots = [piece for piece, _ in pieces]
    places = [place(level) for level in range(levels)]

    barrier = pltpu.get_barrier_semaphore()
    distinct = range(min(levels, nbits))
    for level in distinct:
        pl.semaphore_signal(barrier, inc=1, device_id=places[level][1], device_id_type=MESH)

    def load_source(k):
        cols = pl.ds(k * WIDTH, WIDTH)
        return pltpu.make_async_copy(sources.at[:, cols], src.at[k], src_sem.at[k])

    def load_weights(level):
        return pltpu.make_async_copy(transfer.at[level], weights.at[level], load_sem.at[level])

    load_inward = pltpu.make_async_copy(coeff_in, inward, load_sem.at[levels])

    def rows_of(piece, side):
        _, half = piece
        height = rank if half is None else rank // 2
        start = 0 if half is None else half * rank
        return pl.ds(pl.multiple_of(start + side * height, height), height)

    def exchange(level, piece):
        side, partner = places[level]
        mine = pairs.at[level, piece[0], rows_of(piece, side), :]
        slot = slots.index(piece)
        return pltpu.make_async_remote_copy(
            src_ref=mine,
            dst_ref=mine,
            send_sem=send_sem.at[0],
            recv_sem=recv_sem.at[level, slot],
            device_id=partner,
            device_id_type=MESH,
        )

    left = lax.broadcasted_iota(jnp.int32, (rank // 2, WIDTH), 1) < WIDTH // 2

    def swap(total):
        return pltpu.roll(total, WIDTH // 2, axis=1)

    def pack(level, piece, top, bottom):
        side = places[level][0]
        packed = jnp.where(left, top, bottom).astype(jnp.bfloat16)
        pairs[level, piece[0], rows_of(piece, side), :] = packed

    def product(level, piece):
        k, half = piece
        if half is None:
            return jnp.dot(weights[level], pairs[level, k], preferred_element_type=jnp.float32)
        q = rank // 2
        held = pairs[level, k, half * rank : (half + 1) * rank, :]
        first = jnp.concatenate([weights[level, :, :q], weights[level, :, 2 * q : 3 * q]], axis=1)
        second = jnp.concatenate([weights[level, :, q : 2 * q], weights[level, :, 3 * q :]], axis=1)
        return (
            jnp.dot(first, held, preferred_element_type=jnp.float32),
            jnp.dot(second, held, preferred_element_type=jnp.float32),
        )

    compressed, written = set(), set()

    def compress(piece):
        k, half = piece
        if k in compressed:
            return
        compressed.add(k)
        load_source(k).wait()
        total = jnp.dot(
            inward[...], src[k].astype(jnp.bfloat16), preferred_element_type=jnp.float32
        )
        if half is None:
            pairs[0, k, rows_of(piece, places[0][0]), :] = total.astype(jnp.bfloat16)
        else:
            top, bottom = total[: rank // 2], total[rank // 2 :]
            pack(0, (k, 0), top, swap(bottom))
            pack(0, (k, 1), swap(top), bottom)

    def stage(s, piece):
        k, half = piece
        if s == 0:
            compress(piece)
        else:
            exchange(s - 1, piece).wait_recv()
            total = product(s - 1, piece)
        if s == levels:
            cols = slice(k * WIDTH, (k + 1) * WIDTH)
            if half is not None:
                one, two = total
                total = one + swap(two) if half == 0 else swap(one) + two
                if k in written:
                    whole = lax.broadcasted_iota(jnp.int32, (rank, WIDTH), 1) < WIDTH // 2
                    other = state[:, cols].astype(jnp.float32)
                    total = jnp.where(whole == (half == 0), total, other)
                written.add(k)
            state[:, cols] = total.astype(jnp.bfloat16)
            return
        if s > 0:
            if half is None:
                pairs[s, k, rows_of(piece, places[s][0]), :] = total.astype(jnp.bfloat16)
            else:
                one, two = total
                q = rank // 2
                pack(s, piece, one[:q] + swap(two[:q]), swap(one[q:]) + two[q:])
        if entered:
            entered.pop()
            pl.semaphore_wait(barrier, len(distinct))
        exchange(s, piece).start()

    entered = [True]
    turns = sorted((start + LAGS[s], -s, i) for i, (_, start) in enumerate(pieces) for s in range(levels + 1))

    load_inward.start()
    order = []
    for _, minus, i in turns:
        k = pieces[i][0][0]
        if minus == 0 and k not in order:
            order.append(k)
    for k in order:
        load_source(k).start()
    for level in range(levels):
        load_weights(level).start()

    ready = set()
    for _, minus, i in turns:
        s = -minus
        if s not in ready:
            ready.add(s)
            if s == 0:
                load_inward.wait()
            else:
                load_weights(s - 1).wait()
        stage(s, pieces[i][0])

    sent = pairs.at[:, :, pl.ds(0, rank), :]
    pltpu.make_async_copy(sent, sent, send_sem.at[0]).wait()


def expand(state, outward, targets, held, out_sem):
    width = 256
    stores = []
    for k in range(state.shape[1] // width):
        cols = pl.ds(k * width, width)
        held[:, cols] = jnp.dot(outward[...], state[:, cols], preferred_element_type=jnp.float32)
        store = pltpu.make_async_copy(held.at[:, cols], targets.at[:, cols], out_sem.at[k])
        store.start()
        stores.append(store)
    for store in stores:
        store.wait()


def body(sources, coeff_in, transfer, coeff_out):
    low_bits = lax.axis_size("gx").bit_length() - 1
    nbits = low_bits + lax.axis_size("gy").bit_length() - 1
    levels, rank = transfer.shape[0], coeff_in.shape[2]
    leaf, cols = sources.shape[2:]
    blocks = cols // WIDTH
    slots = len(timetable(blocks))
    state = pl.pallas_call(
        functools.partial(kernel, low_bits, nbits),
        out_shape=pltpu.VMEM((rank, cols), jnp.bfloat16),
        in_specs=[pl.BlockSpec(memory_space=pl.ANY)] * 3,
        out_specs=pl.BlockSpec(memory_space=pltpu.VMEM),
        scratch_shapes=[
            pltpu.VMEM((blocks, leaf, WIDTH), jnp.float32),
            pltpu.VMEM((rank, leaf), jnp.bfloat16),
            pltpu.VMEM((levels, rank, 2 * rank), jnp.bfloat16),
            pltpu.VMEM((levels, blocks, 2 * rank, WIDTH), jnp.bfloat16),
            pltpu.SemaphoreType.DMA((levels + 1,)),
            pltpu.SemaphoreType.DMA((blocks,)),
            pltpu.SemaphoreType.DMA((1,)),
            pltpu.SemaphoreType.DMA((levels, slots)),
        ],
        compiler_params=pltpu.CompilerParams(collective_id=0, has_side_effects=True),
        name="butterfly",
    )(sources[0, 0], coeff_in[0, 0], transfer[:, 0, 0])
    result = pl.pallas_call(
        expand,
        out_shape=jax.ShapeDtypeStruct((leaf, cols), jnp.float32),
        in_specs=[pl.BlockSpec(memory_space=pltpu.VMEM)] * 2,
        out_specs=pl.BlockSpec(memory_space=pl.ANY),
        scratch_shapes=[
            pltpu.VMEM((leaf, cols), jnp.float32),
            pltpu.SemaphoreType.DMA((cols // 256,)),
        ],
        name="expand",
    )(
        pltpu.with_memory_space_constraint(state, pltpu.VMEM),
        pltpu.with_memory_space_constraint(coeff_out[0, 0], pltpu.VMEM),
    )
    return result[None, None]


def solution(mesh):
    placed = (
        P("gy", "gx", None, None),
        P("gy", "gx", None, None),
        P(None, "gy", "gx", None, None),
        P("gy", "gx", None, None),
    )
    return jax.shard_map(
        body, mesh=mesh, in_specs=placed, out_specs=P("gy", "gx", None, None), check_vma=False
    )
```

```python
import functools

import jax
import jax.numpy as jnp
from jax import lax
from jax.experimental import pallas as pl
from jax.experimental.pallas import tpu as pltpu
from jax.sharding import PartitionSpec as P

MESH = pl.DeviceIdType.MESH
WIDTH = 128
LAGS = (10.7, 15.34, 19.14, 21.59, 24.19, 25.91, 30.63, 35.05, 56.81)
PIECES = (
    ((0, 0), -9.37),
    ((1, None), -6.62),
    ((2, None), -3.27),
    ((3, None), -4.44),
    ((4, None), -1.36),
    ((5, None), 3.62),
    ((6, None), 0.5),
    ((7, 0), 5.26),
    ((7, 1), 6.61),
    ((0, 1), 3.14),
)


def timetable(blocks):
    if blocks == 1 + max(k for (k, _), _ in PIECES):
        return PIECES
    return [((k, None), 1.5 * k) for k in range(blocks)]


def kernel(
    low_bits,
    nbits,
    sources,
    coeff_in,
    transfer,
    state,
    src,
    inward,
    weights,
    pairs,
    load_sem,
    src_sem,
    send_sem,
    recv_sem,
):
    levels = transfer.shape[0]
    rank = coeff_in.shape[0]
    blocks = sources.shape[1] // WIDTH
    axes = {"gx": lax.axis_index("gx"), "gy": lax.axis_index("gy")}

    def place(level):
        bit = nbits - 1 - level % nbits
        axis, mask = ("gx", 2**bit) if bit < low_bits else ("gy", 2 ** (bit - low_bits))
        index = axes[axis]
        side = index // mask % 2
        return side, {axis: index + mask * (1 - 2 * side)}

    pieces = timetable(blocks)
    slots = [piece for piece, _ in pieces]
    places = [place(level) for level in range(levels)]

    barrier = pltpu.get_barrier_semaphore()
    distinct = range(min(levels, nbits))
    for level in distinct:
        pl.semaphore_signal(barrier, inc=1, device_id=places[level][1], device_id_type=MESH)

    def load_source(k):
        cols = pl.ds(k * WIDTH, WIDTH)
        return pltpu.make_async_copy(sources.at[:, cols], src.at[k], src_sem.at[k])

    def load_weights(level):
        return pltpu.make_async_copy(transfer.at[level], weights.at[level], load_sem.at[level])

    load_inward = pltpu.make_async_copy(coeff_in, inward, load_sem.at[levels])

    def rows_of(piece, side):
        _, half = piece
        height = rank if half is None else rank // 2
        start = 0 if half is None else half * rank
        return pl.ds(pl.multiple_of(start + side * height, height), height)

    def exchange(level, piece):
        side, partner = places[level]
        mine = pairs.at[level, piece[0], rows_of(piece, side), :]
        slot = slots.index(piece)
        return pltpu.make_async_remote_copy(
            src_ref=mine,
            dst_ref=mine,
            send_sem=send_sem.at[0],
            recv_sem=recv_sem.at[level, slot],
            device_id=partner,
            device_id_type=MESH,
        )

    left = lax.broadcasted_iota(jnp.int32, (rank // 2, WIDTH), 1) < WIDTH // 2

    def swap(total):
        return pltpu.roll(total, WIDTH // 2, axis=1)

    def pack(level, piece, top, bottom):
        side = places[level][0]
        packed = jnp.where(left, top, bottom).astype(jnp.bfloat16)
        pairs[level, piece[0], rows_of(piece, side), :] = packed

    def product(level, piece):
        k, half = piece
        if half is None:
            return jnp.dot(weights[level], pairs[level, k], preferred_element_type=jnp.float32)
        q = rank // 2
        held = pairs[level, k, half * rank : (half + 1) * rank, :]
        first = jnp.concatenate([weights[level, :, :q], weights[level, :, 2 * q : 3 * q]], axis=1)
        second = jnp.concatenate([weights[level, :, q : 2 * q], weights[level, :, 3 * q :]], axis=1)
        return (
            jnp.dot(first, held, preferred_element_type=jnp.float32),
            jnp.dot(second, held, preferred_element_type=jnp.float32),
        )

    compressed, written = set(), set()

    def compress(piece):
        k, half = piece
        if k in compressed:
            return
        compressed.add(k)
        load_source(k).wait()
        total = jnp.dot(
            inward[...], src[k].astype(jnp.bfloat16), preferred_element_type=jnp.float32
        )
        if half is None:
            pairs[0, k, rows_of(piece, places[0][0]), :] = total.astype(jnp.bfloat16)
        else:
            top, bottom = total[: rank // 2], total[rank // 2 :]
            pack(0, (k, 0), top, swap(bottom))
            pack(0, (k, 1), swap(top), bottom)

    def stage(s, piece):
        k, half = piece
        if s == 0:
            compress(piece)
        else:
            exchange(s - 1, piece).wait_recv()
            total = product(s - 1, piece)
        if s == levels:
            cols = slice(k * WIDTH, (k + 1) * WIDTH)
            if half is not None:
                one, two = total
                total = one + swap(two) if half == 0 else swap(one) + two
                if k in written:
                    whole = lax.broadcasted_iota(jnp.int32, (rank, WIDTH), 1) < WIDTH // 2
                    other = state[:, cols].astype(jnp.float32)
                    total = jnp.where(whole == (half == 0), total, other)
                written.add(k)
            state[:, cols] = total.astype(jnp.bfloat16)
            return
        if s > 0:
            if half is None:
                pairs[s, k, rows_of(piece, places[s][0]), :] = total.astype(jnp.bfloat16)
            else:
                one, two = total
                q = rank // 2
                pack(s, piece, one[:q] + swap(two[:q]), swap(one[q:]) + two[q:])
        if entered:
            entered.pop()
            pl.semaphore_wait(barrier, len(distinct))
        exchange(s, piece).start()

    entered = [True]
    turns = sorted((start + LAGS[s], -s, i) for i, (_, start) in enumerate(pieces) for s in range(levels + 1))

    load_inward.start()
    order = []
    for _, minus, i in turns:
        k = pieces[i][0][0]
        if minus == 0 and k not in order:
            order.append(k)
    for k in order:
        load_source(k).start()
    for level in range(levels):
        load_weights(level).start()

    ready = set()
    for _, minus, i in turns:
        s = -minus
        if s not in ready:
            ready.add(s)
            if s == 0:
                load_inward.wait()
            else:
                load_weights(s - 1).wait()
        stage(s, pieces[i][0])

    sent = pairs.at[:, :, pl.ds(0, rank), :]
    pltpu.make_async_copy(sent, sent, send_sem.at[0]).wait()


def expand(state, outward, targets, held, out_sem):
    width = 256
    stores = []
    for k in range(state.shape[1] // width):
        cols = pl.ds(k * width, width)
        held[:, cols] = jnp.dot(outward[...], state[:, cols], preferred_element_type=jnp.float32)
        store = pltpu.make_async_copy(held.at[:, cols], targets.at[:, cols], out_sem.at[k])
        store.start()
        stores.append(store)
    for store in stores:
        store.wait()


def body(sources, coeff_in, transfer, coeff_out):
    low_bits = lax.axis_size("gx").bit_length() - 1
    nbits = low_bits + lax.axis_size("gy").bit_length() - 1
    levels, rank = transfer.shape[0], coeff_in.shape[2]
    leaf, cols = sources.shape[2:]
    blocks = cols // WIDTH
    slots = len(timetable(blocks))
    state = pl.pallas_call(
        functools.partial(kernel, low_bits, nbits),
        out_shape=pltpu.VMEM((rank, cols), jnp.bfloat16),
        in_specs=[pl.BlockSpec(memory_space=pl.ANY)] * 3,
        out_specs=pl.BlockSpec(memory_space=pltpu.VMEM),
        scratch_shapes=[
            pltpu.VMEM((blocks, leaf, WIDTH), jnp.float32),
            pltpu.VMEM((rank, leaf), jnp.bfloat16),
            pltpu.VMEM((levels, rank, 2 * rank), jnp.bfloat16),
            pltpu.VMEM((levels, blocks, 2 * rank, WIDTH), jnp.bfloat16),
            pltpu.SemaphoreType.DMA((levels + 1,)),
            pltpu.SemaphoreType.DMA((blocks,)),
            pltpu.SemaphoreType.DMA((1,)),
            pltpu.SemaphoreType.DMA((levels, slots)),
        ],
        compiler_params=pltpu.CompilerParams(collective_id=0, has_side_effects=True),
        name="butterfly",
    )(sources[0, 0], coeff_in[0, 0], transfer[:, 0, 0])
    result = pl.pallas_call(
        expand,
        out_shape=jax.ShapeDtypeStruct((leaf, cols), jnp.float32),
        in_specs=[pl.BlockSpec(memory_space=pltpu.VMEM)] * 2,
        out_specs=pl.BlockSpec(memory_space=pl.ANY),
        scratch_shapes=[
            pltpu.VMEM((leaf, cols), jnp.float32),
            pltpu.SemaphoreType.DMA((cols // 256,)),
        ],
        name="expand",
    )(
        pltpu.with_memory_space_constraint(state, pltpu.VMEM),
        pltpu.with_memory_space_constraint(coeff_out[0, 0], pltpu.VMEM),
    )
    return result[None, None]


def solution(mesh):
    placed = (
        P("gy", "gx", None, None),
        P("gy", "gx", None, None),
        P(None, "gy", "gx", None, None),
        P("gy", "gx", None, None),
    )
    return jax.shard_map(
        body, mesh=mesh, in_specs=placed, out_specs=P("gy", "gx", None, None), check_vma=False
    )
```

```python
import functools

import jax
import jax.numpy as jnp
from jax import lax
from jax.experimental import pallas as pl
from jax.experimental.pallas import tpu as pltpu
from jax.sharding import PartitionSpec as P

MESH = pl.DeviceIdType.MESH
WIDTH = 128
LAGS = (-0.96, 4.82, 10.4, 13.61, 16.65, 17.98, 23.93, 30.41, 37.38)
PIECES = (
    ((0, 0), 4.97),
    ((1, 0), 2.47),
    ((2, None), 3.21),
    ((3, None), 8.32),
    ((4, None), 9.56),
    ((5, None), 11.73),
    ((6, None), 14.78),
    ((7, None), 18.77),
    ((0, 1), 16.34),
    ((1, 1), 19.79),
)


def timetable(blocks):
    if blocks == 1 + max(k for (k, _), _ in PIECES):
        return PIECES
    return [((k, None), 1.5 * k) for k in range(blocks)]


def kernel(
    low_bits,
    nbits,
    sources,
    coeff_in,
    transfer,
    state,
    src,
    inward,
    weights,
    pairs,
    load_sem,
    src_sem,
    send_sem,
    recv_sem,
):
    levels = transfer.shape[0]
    rank = coeff_in.shape[0]
    blocks = sources.shape[1] // WIDTH
    axes = {"gx": lax.axis_index("gx"), "gy": lax.axis_index("gy")}

    def place(level):
        bit = nbits - 1 - level % nbits
        axis, mask = ("gx", 2**bit) if bit < low_bits else ("gy", 2 ** (bit - low_bits))
        index = axes[axis]
        side = index // mask % 2
        return side, {axis: index + mask * (1 - 2 * side)}

    pieces = timetable(blocks)
    slots = [piece for piece, _ in pieces]
    turns = sorted((start + LAGS[s], -s, i) for i, (_, start) in enumerate(pieces) for s in range(levels + 1))
    order = []
    for _, minus, i in turns:
        k = pieces[i][0][0]
        if minus == 0 and k not in order:
            order.append(k)
    places = [place(level) for level in range(levels)]

    barrier = pltpu.get_barrier_semaphore()
    distinct = range(min(levels, nbits))
    for level in distinct:
        pl.semaphore_signal(barrier, inc=1, device_id=places[level][1], device_id_type=MESH)

    def load_source(k):
        cols = pl.ds(k * WIDTH, WIDTH)
        return pltpu.make_async_copy(sources.at[:, cols], src.at[k], src_sem.at[min(order.index(k), 2)])

    def load_weights(level):
        return pltpu.make_async_copy(transfer.at[level], weights.at[level], load_sem.at[min(level, 2)])

    load_inward = pltpu.make_async_copy(coeff_in, inward, load_sem.at[3])

    held = set()

    def wait_once(key, load, rest, sem):
        if key[:2] not in held:
            held.add(key[:2])
            if key[1] < 2:
                load(key[2]).wait()
            else:
                pltpu.make_async_copy(rest, rest, sem).wait()

    def need_source(k):
        i = min(order.index(k), 2)
        wait_once(("source", i, k), load_source, src.at[pl.ds(0, max(blocks - 2, 1))], src_sem.at[i])

    def need_weights(level):
        i = min(level, 2)
        wait_once(("weights", i, level), load_weights, weights.at[2:], load_sem.at[i])

    def rows_of(piece, side):
        _, half = piece
        height = rank if half is None else rank // 2
        start = 0 if half is None else half * rank
        return pl.ds(pl.multiple_of(start + side * height, height), height)

    def exchange(level, piece):
        side, partner = places[level]
        mine = pairs.at[level, piece[0], rows_of(piece, side), :]
        slot = slots.index(piece)
        return pltpu.make_async_remote_copy(
            src_ref=mine,
            dst_ref=mine,
            send_sem=send_sem.at[0],
            recv_sem=recv_sem.at[level % (nbits + 1), slot],
            device_id=partner,
            device_id_type=MESH,
        )

    left = lax.broadcasted_iota(jnp.int32, (rank // 2, WIDTH), 1) < WIDTH // 2

    def swap(total):
        return pltpu.roll(total, WIDTH // 2, axis=1)

    def pack(level, piece, top, bottom):
        side = places[level][0]
        packed = jnp.where(left, top, bottom).astype(jnp.bfloat16)
        pairs[level, piece[0], rows_of(piece, side), :] = packed

    def product(level, piece):
        k, half = piece
        if half is None:
            return jnp.dot(weights[level], pairs[level, k], preferred_element_type=jnp.float32)
        q = rank // 2
        held = pairs[level, k, half * rank : (half + 1) * rank, :]
        first = jnp.concatenate([weights[level, :, :q], weights[level, :, 2 * q : 3 * q]], axis=1)
        second = jnp.concatenate([weights[level, :, q : 2 * q], weights[level, :, 3 * q :]], axis=1)
        return (
            jnp.dot(first, held, preferred_element_type=jnp.float32),
            jnp.dot(second, held, preferred_element_type=jnp.float32),
        )

    compressed, written = set(), set()

    def compress(piece):
        k, half = piece
        if k in compressed:
            return
        compressed.add(k)
        need_source(k)
        total = jnp.dot(
            inward[...], src[k].astype(jnp.bfloat16), preferred_element_type=jnp.float32
        )
        if half is None:
            pairs[0, k, rows_of(piece, places[0][0]), :] = total.astype(jnp.bfloat16)
        else:
            top, bottom = total[: rank // 2], total[rank // 2 :]
            pack(0, (k, 0), top, swap(bottom))
            pack(0, (k, 1), swap(top), bottom)

    def stage(s, piece):
        k, half = piece
        if s == 0:
            compress(piece)
        else:
            exchange(s - 1, piece).wait_recv()
            total = product(s - 1, piece)
        if s == levels:
            cols = slice(k * WIDTH, (k + 1) * WIDTH)
            if half is not None:
                one, two = total
                total = one + swap(two) if half == 0 else swap(one) + two
                if k in written:
                    whole = lax.broadcasted_iota(jnp.int32, (rank, WIDTH), 1) < WIDTH // 2
                    other = state[:, cols].astype(jnp.float32)
                    total = jnp.where(whole == (half == 0), total, other)
                written.add(k)
            state[:, cols] = total.astype(jnp.bfloat16)
            return
        if s > 0:
            if half is None:
                pairs[s, k, rows_of(piece, places[s][0]), :] = total.astype(jnp.bfloat16)
            else:
                one, two = total
                q = rank // 2
                pack(s, piece, one[:q] + swap(two[:q]), swap(one[q:]) + two[q:])
        if entered:
            entered.pop()
            pl.semaphore_wait(barrier, len(distinct))
        exchange(s, piece).start()

    entered = [True]

    load_inward.start()
    for k in order:
        load_source(k).start()
    for level in range(levels):
        load_weights(level).start()

    ready = set()
    for _, minus, i in turns:
        s = -minus
        if s not in ready:
            ready.add(s)
            if s == 0:
                load_inward.wait()
            else:
                need_weights(s - 1)
        stage(s, pieces[i][0])

    sent = pairs.at[:, :, pl.ds(0, rank), :]
    pltpu.make_async_copy(sent, sent, send_sem.at[0]).wait()


def expand(state, outward, targets, held, out_sem):
    width = 256
    stores = []
    for k in range(state.shape[1] // width):
        cols = pl.ds(k * width, width)
        held[:, cols] = jnp.dot(outward[...], state[:, cols], preferred_element_type=jnp.float32)
        store = pltpu.make_async_copy(held.at[:, cols], targets.at[:, cols], out_sem.at[k])
        store.start()
        stores.append(store)
    for store in stores:
        store.wait()


def body(sources, coeff_in, transfer, coeff_out):
    low_bits = lax.axis_size("gx").bit_length() - 1
    nbits = low_bits + lax.axis_size("gy").bit_length() - 1
    levels, rank = transfer.shape[0], coeff_in.shape[2]
    leaf, cols = sources.shape[2:]
    blocks = cols // WIDTH
    slots = len(timetable(blocks))
    state = pl.pallas_call(
        functools.partial(kernel, low_bits, nbits),
        out_shape=pltpu.VMEM((rank, cols), jnp.bfloat16),
        in_specs=[pl.BlockSpec(memory_space=pl.ANY)] * 3,
        out_specs=pl.BlockSpec(memory_space=pltpu.VMEM),
        scratch_shapes=[
            pltpu.VMEM((blocks, leaf, WIDTH), jnp.float32),
            pltpu.VMEM((rank, leaf), jnp.bfloat16),
            pltpu.VMEM((levels, rank, 2 * rank), jnp.bfloat16),
            pltpu.VMEM((levels, blocks, 2 * rank, WIDTH), jnp.bfloat16),
            pltpu.SemaphoreType.DMA((4,)),
            pltpu.SemaphoreType.DMA((3,)),
            pltpu.SemaphoreType.DMA((1,)),
            pltpu.SemaphoreType.DMA((min(levels, nbits + 1), slots)),
        ],
        compiler_params=pltpu.CompilerParams(collective_id=0, has_side_effects=True),
        name="butterfly",
    )(sources[0, 0], coeff_in[0, 0], transfer[:, 0, 0])
    result = pl.pallas_call(
        expand,
        out_shape=jax.ShapeDtypeStruct((leaf, cols), jnp.float32),
        in_specs=[pl.BlockSpec(memory_space=pltpu.VMEM)] * 2,
        out_specs=pl.BlockSpec(memory_space=pl.ANY),
        scratch_shapes=[
            pltpu.VMEM((leaf, cols), jnp.float32),
            pltpu.SemaphoreType.DMA((cols // 256,)),
        ],
        name="expand",
    )(
        pltpu.with_memory_space_constraint(state, pltpu.VMEM),
        pltpu.with_memory_space_constraint(coeff_out[0, 0], pltpu.VMEM),
    )
    return result[None, None]


def solution(mesh):
    placed = (
        P("gy", "gx", None, None),
        P("gy", "gx", None, None),
        P(None, "gy", "gx", None, None),
        P("gy", "gx", None, None),
    )
    return jax.shard_map(
        body, mesh=mesh, in_specs=placed, out_specs=P("gy", "gx", None, None), check_vma=False
    )
```

```python
import functools

import jax
import jax.numpy as jnp
from jax import lax
from jax.experimental import pallas as pl
from jax.experimental.pallas import tpu as pltpu
from jax.sharding import PartitionSpec as P

MESH = pl.DeviceIdType.MESH
WIDTH = 128
LAGS = (-0.96, 4.82, 10.4, 13.61, 16.65, 17.98, 23.93, 30.41, 37.38)
PIECES = (
    ((0, 0), 4.97),
    ((1, 0), 2.47),
    ((2, None), 3.21),
    ((3, None), 8.32),
    ((4, None), 9.56),
    ((5, None), 11.73),
    ((6, None), 14.78),
    ((7, None), 18.77),
    ((0, 1), 16.34),
    ((1, 1), 19.79),
)


def timetable(blocks):
    if blocks == 1 + max(k for (k, _), _ in PIECES):
        return PIECES
    return [((k, None), 1.5 * k) for k in range(blocks)]


def kernel(
    low_bits,
    nbits,
    sources,
    coeff_in,
    transfer,
    state,
    src,
    inward,
    weights,
    pairs,
    load_sem,
    src_sem,
    send_sem,
    recv_sem,
):
    levels = transfer.shape[0]
    rank = coeff_in.shape[0]
    blocks = sources.shape[1] // WIDTH
    axes = {"gx": lax.axis_index("gx"), "gy": lax.axis_index("gy")}

    def place(level):
        bit = nbits - 1 - level % nbits
        axis, mask = ("gx", 2**bit) if bit < low_bits else ("gy", 2 ** (bit - low_bits))
        index = axes[axis]
        side = index // mask % 2
        return side, {axis: index + mask * (1 - 2 * side)}

    pieces = timetable(blocks)
    slots = [piece for piece, _ in pieces]
    turns = sorted((start + LAGS[s], -s, i) for i, (_, start) in enumerate(pieces) for s in range(levels + 1))
    order = []
    for _, minus, i in turns:
        k = pieces[i][0][0]
        if minus == 0 and k not in order:
            order.append(k)
    places = [place(level) for level in range(levels)]

    barrier = pltpu.get_barrier_semaphore()
    distinct = range(min(levels, nbits))
    for level in distinct:
        pl.semaphore_signal(barrier, inc=1, device_id=places[level][1], device_id_type=MESH)

    def load_source(k):
        cols = pl.ds(k * WIDTH, WIDTH)
        return pltpu.make_async_copy(sources.at[:, cols], src.at[k], src_sem.at[min(order.index(k), 2)])

    def load_weights(level):
        return pltpu.make_async_copy(transfer.at[level], weights.at[level], load_sem.at[min(level, 2)])

    load_inward = pltpu.make_async_copy(coeff_in, inward, load_sem.at[3])

    held = set()

    def wait_once(key, load, rest, sem):
        if key[:2] not in held:
            held.add(key[:2])
            if key[1] < 2:
                load(key[2]).wait()
            else:
                pltpu.make_async_copy(rest, rest, sem).wait()

    def need_source(k):
        i = min(order.index(k), 2)
        wait_once(("source", i, k), load_source, src.at[pl.ds(0, max(blocks - 2, 1))], src_sem.at[i])

    def need_weights(level):
        i = min(level, 2)
        wait_once(("weights", i, level), load_weights, weights.at[2:], load_sem.at[i])

    def rows_of(piece, side):
        _, half = piece
        height = rank if half is None else rank // 2
        start = 0 if half is None else half * rank
        return pl.ds(pl.multiple_of(start + side * height, height), height)

    def exchange(level, piece):
        side, partner = places[level]
        mine = pairs.at[level, piece[0], rows_of(piece, side), :]
        slot = slots.index(piece)
        return pltpu.make_async_remote_copy(
            src_ref=mine,
            dst_ref=mine,
            send_sem=send_sem.at[0],
            recv_sem=recv_sem.at[level % (nbits + 1), slot],
            device_id=partner,
            device_id_type=MESH,
        )

    left = lax.broadcasted_iota(jnp.int32, (rank // 2, WIDTH), 1) < WIDTH // 2

    def swap(total):
        return pltpu.roll(total, WIDTH // 2, axis=1)

    def pack(level, piece, top, bottom):
        side = places[level][0]
        packed = jnp.where(left, top, bottom).astype(jnp.bfloat16)
        pairs[level, piece[0], rows_of(piece, side), :] = packed

    def product(level, piece):
        k, half = piece
        if half is None:
            return jnp.dot(weights[level], pairs[level, k], preferred_element_type=jnp.float32)
        q = rank // 2
        held = pairs[level, k, half * rank : (half + 1) * rank, :]
        first = jnp.concatenate([weights[level, :, :q], weights[level, :, 2 * q : 3 * q]], axis=1)
        second = jnp.concatenate([weights[level, :, q : 2 * q], weights[level, :, 3 * q :]], axis=1)
        return (
            jnp.dot(first, held, preferred_element_type=jnp.float32),
            jnp.dot(second, held, preferred_element_type=jnp.float32),
        )

    compressed, written = set(), set()

    def compress(piece):
        k, half = piece
        if k in compressed:
            return
        compressed.add(k)
        need_source(k)
        total = jnp.dot(
            inward[...], src[k].astype(jnp.bfloat16), preferred_element_type=jnp.float32
        )
        if half is None:
            pairs[0, k, rows_of(piece, places[0][0]), :] = total.astype(jnp.bfloat16)
        else:
            top, bottom = total[: rank // 2], total[rank // 2 :]
            pack(0, (k, 0), top, swap(bottom))
            pack(0, (k, 1), swap(top), bottom)

    def stage(s, piece):
        k, half = piece
        if s == 0:
            compress(piece)
        else:
            exchange(s - 1, piece).wait_recv()
            total = product(s - 1, piece)
        if s == levels:
            cols = slice(k * WIDTH, (k + 1) * WIDTH)
            if half is not None:
                one, two = total
                total = one + swap(two) if half == 0 else swap(one) + two
                if k in written:
                    whole = lax.broadcasted_iota(jnp.int32, (rank, WIDTH), 1) < WIDTH // 2
                    other = state[:, cols].astype(jnp.float32)
                    total = jnp.where(whole == (half == 0), total, other)
                written.add(k)
            state[:, cols] = total.astype(jnp.bfloat16)
            return
        if s > 0:
            if half is None:
                pairs[s, k, rows_of(piece, places[s][0]), :] = total.astype(jnp.bfloat16)
            else:
                one, two = total
                q = rank // 2
                pack(s, piece, one[:q] + swap(two[:q]), swap(one[q:]) + two[q:])
        if entered:
            entered.pop()
            pl.semaphore_wait(barrier, len(distinct))
        exchange(s, piece).start()

    entered = [True]

    load_inward.start()
    for k in order:
        load_source(k).start()

    for level in range(min(levels, 2)):
        load_weights(level).start()
    ready, fetched = set(), []
    for _, minus, i in turns:
        s = -minus
        if s not in ready:
            ready.add(s)
            if s == 0:
                load_inward.wait()
            else:
                need_weights(s - 1)
        stage(s, pieces[i][0])
        if len(ready) == 1 and not fetched:
            fetched.append(True)
            for level in range(2, levels):
                load_weights(level).start()

    sent = pairs.at[:, :, pl.ds(0, rank), :]
    pltpu.make_async_copy(sent, sent, send_sem.at[0]).wait()


def expand(state, outward, targets, held, out_sem):
    width = 256
    stores = []
    for k in range(state.shape[1] // width):
        cols = pl.ds(k * width, width)
        held[:, cols] = jnp.dot(outward[...], state[:, cols], preferred_element_type=jnp.float32)
        store = pltpu.make_async_copy(held.at[:, cols], targets.at[:, cols], out_sem.at[k])
        store.start()
        stores.append(store)
    for store in stores:
        store.wait()


def body(sources, coeff_in, transfer, coeff_out):
    low_bits = lax.axis_size("gx").bit_length() - 1
    nbits = low_bits + lax.axis_size("gy").bit_length() - 1
    levels, rank = transfer.shape[0], coeff_in.shape[2]
    leaf, cols = sources.shape[2:]
    blocks = cols // WIDTH
    slots = len(timetable(blocks))
    state = pl.pallas_call(
        functools.partial(kernel, low_bits, nbits),
        out_shape=pltpu.VMEM((rank, cols), jnp.bfloat16),
        in_specs=[pl.BlockSpec(memory_space=pl.ANY)] * 3,
        out_specs=pl.BlockSpec(memory_space=pltpu.VMEM),
        scratch_shapes=[
            pltpu.VMEM((blocks, leaf, WIDTH), jnp.float32),
            pltpu.VMEM((rank, leaf), jnp.bfloat16),
            pltpu.VMEM((levels, rank, 2 * rank), jnp.bfloat16),
            pltpu.VMEM((levels, blocks, 2 * rank, WIDTH), jnp.bfloat16),
            pltpu.SemaphoreType.DMA((4,)),
            pltpu.SemaphoreType.DMA((3,)),
            pltpu.SemaphoreType.DMA((1,)),
            pltpu.SemaphoreType.DMA((min(levels, nbits + 1), slots)),
        ],
        compiler_params=pltpu.CompilerParams(collective_id=0, has_side_effects=True),
        name="butterfly",
    )(sources[0, 0], coeff_in[0, 0], transfer[:, 0, 0])
    result = pl.pallas_call(
        expand,
        out_shape=jax.ShapeDtypeStruct((leaf, cols), jnp.float32),
        in_specs=[pl.BlockSpec(memory_space=pltpu.VMEM)] * 2,
        out_specs=pl.BlockSpec(memory_space=pl.ANY),
        scratch_shapes=[
            pltpu.VMEM((leaf, cols), jnp.float32),
            pltpu.SemaphoreType.DMA((cols // 256,)),
        ],
        name="expand",
    )(
        pltpu.with_memory_space_constraint(state, pltpu.VMEM),
        pltpu.with_memory_space_constraint(coeff_out[0, 0], pltpu.VMEM),
    )
    return result[None, None]


def solution(mesh):
    placed = (
        P("gy", "gx", None, None),
        P("gy", "gx", None, None),
        P(None, "gy", "gx", None, None),
        P("gy", "gx", None, None),
    )
    return jax.shard_map(
        body, mesh=mesh, in_specs=placed, out_specs=P("gy", "gx", None, None), check_vma=False
    )
```
